32 devices in a mesh: harm: 4 (over x, core), gx: 8 (over z, y).
Axes of the slice: x: 2, y: 2, z: 4, core: 2. Of those that a mesh axis runs over, the one named last changes fastest.
Arguments:
- states: bfloat16 [16, 16, 5, 2, 8, 128], P('harm', 'gx'), may hold values from -6 to 6
- jacobian: bfloat16 [31, 16, 5, 5, 2, 128], P(None, 'gx'), may hold values from -0.5 to 0.5
- source: bfloat16 [16, 5, 5, 128], P('gx'), may hold values from -2.5 to 2.5
- coupling: int32 [16, 16], replicated, may hold values from 0 to 30
- harmonic_of_slot: int32 [16], replicated, may hold values from 0 to 15, each once
Outputs:
- response: bfloat16 [16, 16, 5, 2, 8, 128], P('harm', 'gx')
The draws below stay inside these ranges and needn't reach their ends.
Inputs may be any that keep to these rules, and one draw needn't show every extreme that they name: `harmonic_of_slot`: each harmonic appears in exactly one slot.
All inputs are finite; a program needn't handle non-finite values.
Results may differ from the reference program's by a relative error of at most 0.0038.
Values may be sent and summed in bfloat16 or wider, within the bound.
No kernel may reach another device: no remote copies, remote signals or barrier semaphores. Data moves between devices by JAX's collectives and lax.ppermute only.
A program may use at most 64 MiB of HBM per device.

```python
import jax
import jax.numpy as jnp
from jax import lax

H = 16
NJ = 31
Y = 128
C = 8
X = 16


def plant(values, rng, smallest, top_value):
    longest = values.shape.index(max(values.shape))
    spots = []
    for shift in (0, 1):
        where = [jax.random.randint(jax.random.fold_in(rng, axis), (), 0, length) for axis, length in enumerate(values.shape)]
        where[longest] = (where[longest] + shift) % values.shape[longest]
        spots.append(tuple(where))
    return values.at[spots[0]].set(smallest).at[spots[1]].set(top_value)


def block_scale(stream_key, dims, shards, least, largest):
    gain, own = 1.0, jax.random.fold_in(stream_key, 6)
    for dim, parts in shards:
        steps = jnp.exp(jax.random.uniform(jax.random.fold_in(own, dim), (parts,), jnp.float32, least / len(shards), largest / len(shards)))
        gain = gain * jnp.repeat(steps, dims[dim] // parts).reshape([-1 if axis == dim else 1 for axis in range(len(dims))])
    return gain


def gaussian(key, shape, spread, limit, cuts=(), held_as=jnp.bfloat16):
    level = block_scale(key, shape, cuts, -0.22, 0.18) if cuts else 1.0
    values = jax.random.normal(key, shape, jnp.float32) * spread * level
    return jnp.minimum(jnp.maximum(values, -limit), limit).astype(held_as)


def setup_inputs(seed: int = 0) -> dict:
    splits = jax.random.split(jax.random.key(seed), 6)
    return {
        "states": gaussian(splits[0], (H, X, 5, 2, C, Y), 1.0, 6.0, ((0, 4), (1, 8))),
        "jacobian": gaussian(splits[1], (NJ, X, 5, 5, 2, Y), 0.08, 0.5, ((1, 8),)),
        "source": gaussian(splits[2], (X, 5, 5, Y), 5 ** -0.5, 2.5, ((0, 8),)),
        "coupling": plant(jax.random.randint(splits[3], (H, H), 0, NJ), jax.random.fold_in(splits[3], 1), 0, NJ - 1).astype(jnp.int32),
        "harmonic_of_slot": jax.random.permutation(splits[4], H).astype(jnp.int32),
    }


def pair_term(jacobian_block, state_block):
    mat_real = jacobian_block[:, :, :, 0].astype(jnp.float32)
    mat_imag = jacobian_block[:, :, :, 1].astype(jnp.float32)
    vec_real = state_block[:, :, 0].astype(jnp.float32)
    vec_imag = state_block[:, :, 1].astype(jnp.float32)

    def contract(matrix, vector):
        return jnp.einsum("xaby,xbcy->xacy", matrix, vector)

    real_part = contract(mat_real, vec_real) - contract(mat_imag, vec_imag)
    imag_part = contract(mat_real, vec_imag) + contract(mat_imag, vec_real)
    return jnp.stack([real_part, imag_part], axis=2)


def reference(states, jacobian, source, coupling, harmonic_of_slot):
    def one_slot(own_slot):
        own_harmonic = harmonic_of_slot[own_slot]
        link_row = coupling[own_harmonic]

        def accumulate(member, carry_sum):
            peer_harmonic = harmonic_of_slot[member]
            link_index = link_row[peer_harmonic]
            return carry_sum + pair_term(jacobian[link_index], states[member])

        zeros_init = jnp.zeros(states.shape[1:], jnp.float32)
        return lax.fori_loop(0, H, accumulate, zeros_init)

    flux_sum = lax.map(one_slot, jnp.arange(H, dtype=jnp.int32))
    flux_field = lax.optimization_barrier(flux_sum.astype(jnp.bfloat16)).astype(jnp.float32)
    ahead_one = jnp.roll(flux_field, -1, axis=1)
    behind_one = jnp.roll(flux_field, 1, axis=1)
    ahead_two = jnp.roll(flux_field, -2, axis=1)
    behind_two = jnp.roll(flux_field, 2, axis=1)
    divergence = (8.0 * (ahead_one - behind_one) - (ahead_two - behind_two)) / 12.0
    spin_rate = (harmonic_of_slot.astype(jnp.float32) / H).reshape(H, 1, 1, 1, 1)
    state_values = states.astype(jnp.float32)
    spin_term = jnp.stack([-spin_rate * state_values[:, :, :, 1], spin_rate * state_values[:, :, :, 0]], axis=3)
    merged = state_values.reshape(H, states.shape[1], 5, 2 * C, Y)
    source_term = jnp.einsum("xaby,sxbky->sxaky", source.astype(jnp.float32), merged).reshape(states.shape)
    return (divergence + spin_term + source_term).astype(jnp.bfloat16)
```

```python
import functools

import jax
import jax.numpy as jnp
from jax import lax
from jax.experimental import pallas as pl
from jax.experimental.pallas import tpu as pltpu
from jax.sharding import PartitionSpec as P

VMEM = pltpu.VMEM
SMEM = pltpu.SMEM
VARS = 5


def row(table, index):
    return table[pl.ds(index, 8, stride=0), :]


def expand(jac_ref, table, sums):
    count = jac_ref.shape[0] // 2
    table[: 2 * count, :] = jac_ref[...].astype(jnp.float32)
    for start in range(0, count, 8):
        size = min(8, count - start)
        real = table[pl.ds(2 * start, size, stride=2), :]
        imag = table[pl.ds(2 * start + 1, size, stride=2), :]
        sums[pl.ds(start, size), :] = real + imag


def flux_block(first_own, first_peer, harm_ref, coup_ref, state_ref, table, sums, own, cell, cells, acc):
    def body(member, acc):
        peer = harm_ref[first_peer + member]
        vec_real, vec_imag, vec_sum = [], [], []
        for b in range(VARS):
            both = state_ref[member, cell, b].astype(jnp.float32)
            vec_real.append(both[0])
            vec_imag.append(both[1])
            vec_sum.append(both[0] + both[1])
        out = []
        for place, slot in enumerate(own):
            link = coup_ref[harm_ref[first_own + slot], peer]
            base = (link * cells + cell) * (VARS * VARS)
            part = list(acc[place])
            for a in range(VARS):
                for b in range(VARS):
                    offset = a * VARS + b
                    part[3 * a] += row(table, 2 * (base + offset)) * vec_real[b]
                    part[3 * a + 1] += row(table, 2 * (base + offset) + 1) * vec_imag[b]
                    part[3 * a + 2] += row(sums, base + offset) * vec_sum[b]
            out.append(tuple(part))
        return tuple(out)

    return lax.fori_loop(0, state_ref.shape[0], body, acc)


def flux_kernel(groups, stage, *refs):
    harm_ref, coup_ref = refs[:2]
    refs = refs[2:]
    harm = lax.axis_index("harm")
    states = refs[: len(groups)]
    refs = refs[len(groups) :]
    if stage == 0:
        jac_ref, out_ref, table, sums = refs
        expand(jac_ref, table, sums)
        start_ref = None
    else:
        table, sums, start_ref, out_ref = refs
    own_count, cells = out_ref.shape[:2]
    width = 2 if own_count % 2 == 0 else 1
    zero = jnp.zeros((8, 128), jnp.float32)

    def chunk(step, _):
        cell = step % cells
        first = (step // cells) * width
        acc = tuple((zero,) * (3 * VARS) for _ in range(width))
        for shift, state_ref in zip(groups, states):
            peer_group = harm ^ shift
            acc = flux_block(
                harm * own_count + first, peer_group * own_count, harm_ref, coup_ref, state_ref,
                table, sums, range(width), cell, cells, acc,
            )
        for place in range(width):
            for a in range(VARS):
                one, two, three = acc[place][3 * a : 3 * a + 3]
                real = one - two
                imag = three - one - two
                if start_ref is not None:
                    real = real + start_ref[first + place, cell, a, 0]
                    imag = imag + start_ref[first + place, cell, a, 1]
                out_ref[first + place, cell, a, 0] = real.astype(out_ref.dtype)
                out_ref[first + place, cell, a, 1] = imag.astype(out_ref.dtype)
        return 0

    lax.fori_loop(0, cells * (own_count // width), chunk, 0)


def final_kernel(harm_total, harm_ref, own_ref, near_ref, far_ref, state_ref, source_ref, out_ref, table):
    own_count, cells = own_ref.shape[:2]
    harm = lax.axis_index("harm")
    gx = lax.axis_index("gx")
    table[: source_ref.shape[0], :] = source_ref[...].astype(jnp.float32)

    def finish(left_ref, right_ref):
        def flux(slot, a, place):
            if place < 0:
                return left_ref[slot, cells + place, a].astype(jnp.float32)
            if place >= cells:
                return right_ref[slot, place - cells, a].astype(jnp.float32)
            return own_ref[slot, place, a].astype(jnp.float32)

        def body(slot, _):
            spin = harm_ref[harm * own_count + slot].astype(jnp.float32) / harm_total
            for cell in range(cells):
                vec = [state_ref[slot, cell, b].astype(jnp.float32) for b in range(VARS)]
                for a in range(VARS):
                    total = (
                        8.0 * (flux(slot, a, cell + 1) - flux(slot, a, cell - 1))
                        - (flux(slot, a, cell + 2) - flux(slot, a, cell - 2))
                    ) / 12.0
                    real, imag = total[0], total[1]
                    real = real - spin * vec[a][1]
                    imag = imag + spin * vec[a][0]
                    for b in range(VARS):
                        weight = row(table, (cell * VARS + a) * VARS + b)
                        real = real + weight * vec[b][0]
                        imag = imag + weight * vec[b][1]
                    out_ref[slot, cell, a, 0] = real.astype(out_ref.dtype)
                    out_ref[slot, cell, a, 1] = imag.astype(out_ref.dtype)
            return 0

        lax.fori_loop(0, own_count, body, 0)

    @pl.when(gx % 2 == 0)
    def _():
        finish(far_ref, near_ref)

    @pl.when(gx % 2 == 1)
    def _():
        finish(near_ref, far_ref)


def call(kernel, out, spaces, scratch, name):
    return pl.pallas_call(
        kernel,
        out_shape=out,
        in_specs=[pl.BlockSpec(memory_space=space) for space in spaces],
        out_specs=jax.tree.map(lambda _: pl.BlockSpec(memory_space=VMEM), out),
        scratch_shapes=scratch,
        name=name,
    )


def shards(states, jacobian, source, coupling, harmonic_of_slot):
    own_count, cells = states.shape[:2]
    harms = lax.axis_size("harm")
    planes = lax.axis_size("gx")
    pairs = jacobian.shape[0] * cells * VARS * VARS

    def swap(block, shift):
        return lax.ppermute(block, "harm", [(i, i ^ shift) for i in range(harms)])

    held = {0: states}
    for shift in range(1, harms):
        low = shift & -shift
        held[shift] = swap(states if shift == low else held[shift ^ low], low if shift != low else shift)
    first = [0, 1]
    rest = [shift for shift in range(2, harms)]
    flat = jacobian.reshape(2 * pairs, 128)
    f32 = jnp.float32
    part, table, sums = call(
        functools.partial(flux_kernel, first, 0),
        (
            jax.ShapeDtypeStruct(states.shape, f32),
            jax.ShapeDtypeStruct((2 * pairs + 8, 128), f32),
            jax.ShapeDtypeStruct((pairs + 8, 128), f32),
        ),
        [SMEM, SMEM] + [VMEM] * 3,
        [],
        "flux_a",
    )(harmonic_of_slot, coupling, *[held[s] for s in first], flat)
    flux = call(
        functools.partial(flux_kernel, rest, 1),
        jax.ShapeDtypeStruct(states.shape, jnp.bfloat16),
        [SMEM, SMEM] + [VMEM] * (len(rest) + 3),
        [],
        "flux_b",
    )(harmonic_of_slot, coupling, *[held[s] for s in rest], table, sums, part)
    near_pairs = [(i, i ^ 1) for i in range(planes)]
    far_pairs = [(i, (i + 1) % planes if i % 2 else (i - 1) % planes) for i in range(planes)]
    far = lax.ppermute(flux, "gx", far_pairs)
    near = lax.ppermute(flux, "gx", near_pairs)
    return call(
        functools.partial(final_kernel, coupling.shape[0]),
        jax.ShapeDtypeStruct(states.shape, jnp.bfloat16),
        [SMEM] + [VMEM] * 5,
        [pltpu.VMEM((cells * VARS * VARS + 8, 128), f32)],
        "finish",
    )(harmonic_of_slot, flux, near, far, states, source.reshape(cells * VARS * VARS, 128))


def solution(mesh):
    return jax.shard_map(
        shards,
        mesh=mesh,
        in_specs=(
            P("harm", "gx", None, None, None, None),
            P(None, "gx", None, None, None, None),
            P("gx", None, None, None),
            P(),
            P(),
        ),
        out_specs=P("harm", "gx", None, None, None, None),
        check_vma=False,
    )
```

```python
import functools

import jax
import jax.numpy as jnp
from jax import lax
from jax.experimental import pallas as pl
from jax.experimental.pallas import tpu as pltpu
from jax.sharding import PartitionSpec as P


VMEM = pltpu.VMEM
SMEM = pltpu.SMEM
HBM = pltpu.HBM
F32 = jnp.float32
VARS = 5
LIMIT = 16 << 20
PIECES = 4


def row(table, index):
    return table[pl.ds(index, 8, stride=0), :]


def flux_block(first_own, first_peer, harm_ref, coup_ref, state_ref, table, sums, own, cell, cells, acc):
    count = state_ref.shape[0]

    def places(member):
        peer = harm_ref[first_peer + member]
        return tuple(
            (coup_ref[harm_ref[first_own + slot], peer] * cells + cell) * (VARS * VARS) for slot in own
        )

    def body(member, carry):
        acc, bases = carry
        following = places(jnp.minimum(member + 1, count - 1))
        out = [list(part) for part in acc]
        for b in range(VARS):
            both = state_ref[member, cell, b].astype(F32)
            real, imag = both[0], both[1]
            total = real + imag
            for part, base in zip(out, bases):
                for a in range(VARS):
                    offset = base + (a * VARS + b)
                    part[3 * a] += row(table, 2 * offset) * real
                    part[3 * a + 1] += row(table, 2 * offset + 1) * imag
                    part[3 * a + 2] += row(sums, offset) * total
        return tuple(tuple(part) for part in out), following

    unroll = 2 if count % 2 == 0 else 1
    return lax.fori_loop(0, count, body, (acc, places(0)), unroll=unroll)[0]


def flux_sum(groups, states, harm_ref, coup_ref, table, sums, start_ref, out_ref):
    harm = lax.axis_index("harm")
    own_count, cells = out_ref.shape[:2]
    width = 2 if own_count % 2 == 0 else 1
    zero = jnp.zeros((8, 128), F32)

    def chunk(step, _):
        cell = step % cells
        first = (step // cells) * width
        acc = tuple((zero,) * (3 * VARS) for _ in range(width))
        for shift, state_ref in zip(groups, states):
            acc = flux_block(
                harm * own_count + first, (harm ^ shift) * own_count, harm_ref, coup_ref, state_ref,
                table, sums, range(width), cell, cells, acc,
            )
        for place in range(width):
            for a in range(VARS):
                one, two, three = acc[place][3 * a : 3 * a + 3]
                real = one - two
                imag = three - one - two
                if start_ref is not None:
                    real = real + start_ref[first + place, cell, a, 0]
                    imag = imag + start_ref[first + place, cell, a, 1]
                out_ref[first + place, cell, a, 0] = real.astype(out_ref.dtype)
                out_ref[first + place, cell, a, 1] = imag.astype(out_ref.dtype)
        return 0

    lax.fori_loop(0, cells * (own_count // width), chunk, 0)


def first_kernel(
    jac_hbm, state_hbm, harm_hbm, coup_hbm, out_ref, table, sums, harm_ref, coup_ref,
    jac, own, jac_sem, sem,
):
    rows = jac_hbm.size // 128
    flat = jac_hbm.reshape(rows, 128)
    step = -(-rows // (16 * PIECES)) * 16
    spans = [(start, min(step, rows - start)) for start in range(0, rows, step)]
    copies = [
        pltpu.make_async_copy(flat.at[pl.ds(start, size)], jac.at[pl.ds(start, size)], jac_sem.at[i])
        for i, (start, size) in enumerate(spans)
    ]
    others = [
        pltpu.make_async_copy(source, target, sem.at[i])
        for i, (source, target) in enumerate(((harm_hbm, harm_ref), (coup_hbm, coup_ref), (state_hbm, own)))
    ]
    for copy in copies + others:
        copy.start()
    for copy, (start, size) in zip(copies, spans):
        copy.wait()
        for at in range(start, start + size, 16):
            table[pl.ds(at, 16), :] = jac[pl.ds(at, 16), :].astype(F32)
        for at in range(start // 2, (start + size) // 2, 8):
            real = table[pl.ds(2 * at, 8, stride=2), :]
            imag = table[pl.ds(2 * at + 1, 8, stride=2), :]
            sums[pl.ds(at, 8), :] = real + imag
    for copy in others:
        copy.wait()
    flux_sum((0,), (own,), harm_ref, coup_ref, table, sums, None, out_ref)


def next_kernel(groups, harm_ref, coup_ref, *refs):
    states = refs[: len(groups)]
    table, sums, start_ref, out_ref = refs[len(groups) :]
    flux_sum(groups, states, harm_ref, coup_ref, table, sums, start_ref, out_ref)


def local_kernel(harm_total, harm_ref, flux_ref, state_ref, source_ref, out_ref, table):
    own_count, cells = flux_ref.shape[:2]
    first = lax.axis_index("harm") * own_count
    table[: source_ref.shape[0], :] = source_ref[...].astype(F32)

    def body(slot, _):
        spin = harm_ref[first + slot].astype(F32) / harm_total
        for cell in range(cells):
            vec = [state_ref[slot, cell, b].astype(F32) for b in range(VARS)]
            for a in range(VARS):
                real = -spin * vec[a][1]
                imag = spin * vec[a][0]
                for step, weight in ((-2, 1 / 12), (-1, -8 / 12), (1, 8 / 12), (2, -1 / 12)):
                    if 0 <= cell + step < cells:
                        other = flux_ref[slot, cell + step, a].astype(F32)
                        real = real + weight * other[0]
                        imag = imag + weight * other[1]
                for b in range(VARS):
                    weight = row(table, (cell * VARS + a) * VARS + b)
                    real = real + weight * vec[b][0]
                    imag = imag + weight * vec[b][1]
                out_ref[slot, cell, a, 0] = real
                out_ref[slot, cell, a, 1] = imag
        return 0

    lax.fori_loop(0, own_count, body, 0)


def final_kernel(local_ref, near_ref, far_ref, out_ref):
    own_count, cells = out_ref.shape[:2]

    def finish(left_ref, right_ref):
        def body(slot, _):
            for a in range(VARS):
                for cell in range(cells):
                    total = local_ref[slot, cell, a]
                    for step, weight in ((-2, 1 / 12), (-1, -8 / 12), (1, 8 / 12), (2, -1 / 12)):
                        place = cell + step
                        if place < 0:
                            total = total + weight * left_ref[slot, cells + place, a].astype(F32)
                        elif place >= cells:
                            total = total + weight * right_ref[slot, place - cells, a].astype(F32)
                    out_ref[slot, cell, a] = total.astype(out_ref.dtype)
            return 0

        lax.fori_loop(0, own_count, body, 0)

    even = lax.axis_index("gx") % 2 == 0

    @pl.when(even)
    def _():
        finish(far_ref, near_ref)

    @pl.when(jnp.logical_not(even))
    def _():
        finish(near_ref, far_ref)


def call(kernel, out, spaces, flops, scratch=()):
    return pl.pallas_call(
        kernel,
        out_shape=out,
        in_specs=[pl.BlockSpec(memory_space=space) for space in spaces],
        out_specs=jax.tree.map(lambda x: pl.BlockSpec(memory_space=getattr(x, 'memory_space', VMEM)), out),
        scratch_shapes=scratch,
        compiler_params=pltpu.CompilerParams(vmem_limit_bytes=LIMIT),
        cost_estimate=pl.CostEstimate(flops=flops, bytes_accessed=0, transcendentals=0),
    )


def body(states, jacobian, source, coupling, harmonic_of_slot):
    shape = states.shape
    own_count, cells = shape[:2]
    harms = lax.axis_size("harm")
    planes = lax.axis_size("gx")
    pairs = jacobian.shape[0] * cells * VARS * VARS
    padded = -(-2 * pairs // 16) * 16
    dma = pltpu.SemaphoreType.DMA
    shaped = jax.ShapeDtypeStruct

    def swap(block, shift):
        return lax.ppermute(block, "harm", [(i, i ^ shift) for i in range(harms)])

    work = 2 * VARS * VARS * 6 * own_count * states.size // (2 * VARS)
    even = [shift for shift in range(2, harms, 2)]
    odd = [shift + 1 for shift in even]
    partner = swap(states, 1)
    even_states = [swap(states, shift) for shift in even]
    inputs = (jacobian, states, harmonic_of_slot, coupling)
    part, table, sums, held_harm, held_coup = call(
        first_kernel,
        (
            shaped(shape, F32),
            shaped((padded, 128), F32),
            shaped((padded // 2, 128), F32),
            pltpu.SMEM(harmonic_of_slot.shape, jnp.int32),
            pltpu.SMEM(coupling.shape, jnp.int32),
        ),
        [HBM] * 4,
        work,
        [
            pltpu.VMEM((padded, 128), jacobian.dtype),
            pltpu.VMEM(shape, states.dtype),
            dma((PIECES,)),
            dma((3,)),
        ],
    )(*[pltpu.with_memory_space_constraint(x, HBM) for x in inputs])

    def more(groups, blocks, part, dtype):
        return call(
            functools.partial(next_kernel, groups),
            shaped(shape, dtype),
            [SMEM] * 2 + [VMEM] * (len(groups) + 3),
            work * len(groups),
        )(held_harm, held_coup, *blocks, table, sums, part)

    part = more([1], [partner], part, F32)
    *even_states, part = lax.optimization_barrier((*even_states, part))
    odd_states = [swap(block, 1) for block in even_states]

    part = more(even, even_states, part, F32)
    flux = more(odd, odd_states, part, states.dtype)
    near = lax.ppermute(flux, "gx", [(i, i ^ 1) for i in range(planes)])
    far = lax.ppermute(
        flux, "gx", [(i, (i + 1) % planes if i % 2 else (i - 1) % planes) for i in range(planes)]
    )
    sources = cells * VARS * VARS
    local = call(
        functools.partial(local_kernel, coupling.shape[0]),
        shaped(shape, F32),
        [SMEM] + [VMEM] * 3,
        work // 4,
        [pltpu.VMEM((-(-sources // 8) * 8 + 8, 128), F32)],
    )(held_harm, flux, states, source.reshape(sources, 128))
    return call(final_kernel, shaped(shape, states.dtype), [VMEM] * 3, work // 8)(local, near, far)


def solution(mesh):
    return jax.shard_map(
        body,
        mesh=mesh,
        in_specs=(
            P("harm", "gx", None, None, None, None),
            P(None, "gx", None, None, None, None),
            P("gx", None, None, None),
            P(),
            P(),
        ),
        out_specs=P("harm", "gx", None, None, None, None),
        check_vma=False,
    )
```

```python
import functools

import jax
import jax.numpy as jnp
from jax import lax
from jax.experimental import pallas as pl
from jax.experimental.pallas import tpu as pltpu
from jax.sharding import PartitionSpec as P


VMEM = pltpu.VMEM
SMEM = pltpu.SMEM
HBM = pltpu.HBM
F32 = jnp.float32
VARS = 5
LIMIT = 16 << 20
PIECES = 4


def row(table, index):
    return table[pl.ds(index, 8, stride=0), :]


def flux_block(first_own, first_peer, harm_ref, coup_ref, state_ref, table, sums, own, cell, cells, acc):
    count = state_ref.shape[0]

    def places(member):
        peer = harm_ref[first_peer + member]
        return tuple(
            (coup_ref[harm_ref[first_own + slot], peer] * cells + cell) * (VARS * VARS) for slot in own
        )

    def body(member, carry):
        acc, bases = carry
        following = places(jnp.minimum(member + 1, count - 1))
        out = [list(part) for part in acc]
        for b in range(VARS):
            both = state_ref[member, cell, b].astype(F32)
            real, imag = both[0], both[1]
            total = real + imag
            for part, base in zip(out, bases):
                for a in range(VARS):
                    offset = base + (a * VARS + b)
                    part[3 * a] += row(table, 2 * offset) * real
                    part[3 * a + 1] += row(table, 2 * offset + 1) * imag
                    part[3 * a + 2] += row(sums, offset) * total
        return tuple(tuple(part) for part in out), following

    unroll = 2 if count % 2 == 0 else 1
    return lax.fori_loop(0, count, body, (acc, places(0)), unroll=unroll)[0]


def flux_sum(groups, states, harm_ref, coup_ref, table, sums, start_ref, out_ref):
    harm = lax.axis_index("harm")
    own_count, cells = out_ref.shape[:2]
    width = 2 if own_count % 2 == 0 else 1
    zero = jnp.zeros((8, 128), F32)

    def chunk(step, _):
        cell = step % cells
        first = (step // cells) * width
        acc = tuple((zero,) * (3 * VARS) for _ in range(width))
        for shift, state_ref in zip(groups, states):
            acc = flux_block(
                harm * own_count + first, (harm ^ shift) * own_count, harm_ref, coup_ref, state_ref,
                table, sums, range(width), cell, cells, acc,
            )
        for place in range(width):
            for a in range(VARS):
                one, two, three = acc[place][3 * a : 3 * a + 3]
                real = one - two
                imag = three - one - two
                if start_ref is not None:
                    real = real + start_ref[first + place, cell, a, 0]
                    imag = imag + start_ref[first + place, cell, a, 1]
                out_ref[first + place, cell, a, 0] = real.astype(out_ref.dtype)
                out_ref[first + place, cell, a, 1] = imag.astype(out_ref.dtype)
        return 0

    lax.fori_loop(0, cells * (own_count // width), chunk, 0)


def first_kernel(
    jac_hbm, state_hbm, harm_hbm, coup_hbm, out_ref, table, sums, harm_ref, coup_ref,
    jac, own, jac_sem, sem,
):
    rows = jac_hbm.size // 128
    flat = jac_hbm.reshape(rows, 128)
    step = -(-rows // (16 * PIECES)) * 16
    spans = [(start, min(step, rows - start)) for start in range(0, rows, step)]
    copies = [
        pltpu.make_async_copy(flat.at[pl.ds(start, size)], jac.at[pl.ds(start, size)], jac_sem.at[i])
        for i, (start, size) in enumerate(spans)
    ]
    others = [
        pltpu.make_async_copy(source, target, sem.at[i])
        for i, (source, target) in enumerate(((harm_hbm, harm_ref), (coup_hbm, coup_ref), (state_hbm, own)))
    ]
    for copy in copies + others:
        copy.start()
    for copy, (start, size) in zip(copies, spans):
        copy.wait()
        for at in range(start, start + size, 16):
            table[pl.ds(at, 16), :] = jac[pl.ds(at, 16), :].astype(F32)
        for at in range(start // 2, (start + size) // 2, 8):
            real = table[pl.ds(2 * at, 8, stride=2), :]
            imag = table[pl.ds(2 * at + 1, 8, stride=2), :]
            sums[pl.ds(at, 8), :] = real + imag
    for copy in others:
        copy.wait()
    flux_sum((0,), (own,), harm_ref, coup_ref, table, sums, None, out_ref)


def next_kernel(groups, harm_ref, coup_ref, *refs):
    states = refs[: len(groups)]
    table, sums, start_ref, out_ref = refs[len(groups) :]
    flux_sum(groups, states, harm_ref, coup_ref, table, sums, start_ref, out_ref)


def local_kernel(harm_total, harm_ref, flux_ref, state_ref, source_ref, out_ref, table):
    own_count, cells = flux_ref.shape[:2]
    first = lax.axis_index("harm") * own_count
    table[: source_ref.shape[0], :] = source_ref[...].astype(F32)

    def body(slot, _):
        spin = harm_ref[first + slot].astype(F32) / harm_total
        for cell in range(cells):
            vec = [state_ref[slot, cell, b].astype(F32) for b in range(VARS)]
            for a in range(VARS):
                real = -spin * vec[a][1]
                imag = spin * vec[a][0]
                for step, weight in ((-2, 1 / 12), (-1, -8 / 12), (1, 8 / 12), (2, -1 / 12)):
                    if 0 <= cell + step < cells:
                        other = flux_ref[slot, cell + step, a].astype(F32)
                        real = real + weight * other[0]
                        imag = imag + weight * other[1]
                for b in range(VARS):
                    weight = row(table, (cell * VARS + a) * VARS + b)
                    real = real + weight * vec[b][0]
                    imag = imag + weight * vec[b][1]
                out_ref[slot, cell, a, 0] = real
                out_ref[slot, cell, a, 1] = imag
        return 0

    lax.fori_loop(0, own_count, body, 0)


def final_kernel(local_ref, near_ref, far_ref, out_hbm, out_ref, sem):
    own_count, cells = out_ref.shape[:2]

    def put(slot):
        return pltpu.make_async_copy(out_ref.at[slot], out_hbm.at[slot], sem.at[slot])

    def finish(left_ref, right_ref):
        for slot in range(own_count):
            for a in range(VARS):
                for cell in range(cells):
                    total = local_ref[slot, cell, a]
                    for step, weight in ((-2, 1 / 12), (-1, -8 / 12), (1, 8 / 12), (2, -1 / 12)):
                        place = cell + step
                        if place < 0:
                            total = total + weight * left_ref[slot, cells + place, a].astype(F32)
                        elif place >= cells:
                            total = total + weight * right_ref[slot, place - cells, a].astype(F32)
                    out_ref[slot, cell, a] = total.astype(out_ref.dtype)
            put(slot).start()

    even = lax.axis_index("gx") % 2 == 0

    @pl.when(even)
    def _():
        finish(far_ref, near_ref)

    @pl.when(jnp.logical_not(even))
    def _():
        finish(near_ref, far_ref)

    for slot in range(own_count):
        put(slot).wait()


def call(kernel, out, spaces, flops, scratch=()):
    return pl.pallas_call(
        kernel,
        out_shape=out,
        in_specs=[pl.BlockSpec(memory_space=space) for space in spaces],
        out_specs=jax.tree.map(lambda x: pl.BlockSpec(memory_space=getattr(x, 'memory_space', VMEM)), out),
        scratch_shapes=scratch,
        compiler_params=pltpu.CompilerParams(vmem_limit_bytes=LIMIT),
        cost_estimate=pl.CostEstimate(flops=flops, bytes_accessed=0, transcendentals=0),
    )


def body(states, jacobian, source, coupling, harmonic_of_slot):
    shape = states.shape
    own_count, cells = shape[:2]
    harms = lax.axis_size("harm")
    planes = lax.axis_size("gx")
    pairs = jacobian.shape[0] * cells * VARS * VARS
    padded = -(-2 * pairs // 16) * 16
    dma = pltpu.SemaphoreType.DMA
    shaped = jax.ShapeDtypeStruct

    def swap(block, shift):
        return lax.ppermute(block, "harm", [(i, i ^ shift) for i in range(harms)])

    work = 2 * VARS * VARS * 6 * own_count * states.size // (2 * VARS)
    even = [shift for shift in range(2, harms, 2)]
    odd = [shift + 1 for shift in even]
    partner = swap(states, 1)
    even_states = [swap(states, shift) for shift in even]
    inputs = (jacobian, states, harmonic_of_slot, coupling)
    part, table, sums, held_harm, held_coup = call(
        first_kernel,
        (
            shaped(shape, F32),
            shaped((padded, 128), F32),
            shaped((padded // 2, 128), F32),
            pltpu.SMEM(harmonic_of_slot.shape, jnp.int32),
            pltpu.SMEM(coupling.shape, jnp.int32),
        ),
        [HBM] * 4,
        work,
        [
            pltpu.VMEM((padded, 128), jacobian.dtype),
            pltpu.VMEM(shape, states.dtype),
            dma((PIECES,)),
            dma((3,)),
        ],
    )(*[pltpu.with_memory_space_constraint(x, HBM) for x in inputs])

    def more(groups, blocks, part, dtype):
        return call(
            functools.partial(next_kernel, groups),
            shaped(shape, dtype),
            [SMEM] * 2 + [VMEM] * (len(groups) + 3),
            work * len(groups),
        )(held_harm, held_coup, *blocks, table, sums, part)

    part = more([1], [partner], part, F32)
    *even_states, part = lax.optimization_barrier((*even_states, part))
    odd_states = [swap(block, 1) for block in even_states]

    part = more(even, even_states, part, F32)
    flux = more(odd, odd_states, part, states.dtype)
    near = lax.ppermute(flux, "gx", [(i, i ^ 1) for i in range(planes)])
    far = lax.ppermute(
        flux, "gx", [(i, (i + 1) % planes if i % 2 else (i - 1) % planes) for i in range(planes)]
    )
    sources = cells * VARS * VARS
    local = call(
        functools.partial(local_kernel, coupling.shape[0]),
        shaped(shape, F32),
        [SMEM] + [VMEM] * 3,
        work // 4,
        [pltpu.VMEM((-(-sources // 8) * 8 + 8, 128), F32)],
    )(held_harm, flux, states, source.reshape(sources, 128))
    return call(
        final_kernel,
        HBM(shape, states.dtype),
        [VMEM] * 3,
        work // 8,
        [pltpu.VMEM(shape, states.dtype), dma((own_count,))],
    )(local, near, far)


def solution(mesh):
    return jax.shard_map(
        body,
        mesh=mesh,
        in_specs=(
            P("harm", "gx", None, None, None, None),
            P(None, "gx", None, None, None, None),
            P("gx", None, None, None),
            P(),
            P(),
        ),
        out_specs=P("harm", "gx", None, None, None, None),
        check_vma=False,
    )
```

```python
import functools

import jax
import jax.numpy as jnp
from jax import lax
from jax.experimental import pallas as pl
from jax.experimental.pallas import tpu as pltpu
from jax.sharding import PartitionSpec as P


VMEM = pltpu.VMEM
SMEM = pltpu.SMEM
HBM = pltpu.HBM
F32 = jnp.float32
VARS = 5
LIMIT = 16 << 20
PIECES = 4


def row(table, index):
    return table[pl.ds(index, 8, stride=0), :]


def flux_block(first_own, first_peer, harm_ref, coup_ref, state_ref, table, sums, own, cell, cells, acc):
    count = state_ref.shape[0]

    def places(member):
        peer = harm_ref[first_peer + member]
        return tuple(
            (coup_ref[harm_ref[first_own + slot], peer] * cells + cell) * (VARS * VARS) for slot in own
        )

    def body(member, carry):
        acc, bases = carry
        following = places(jnp.minimum(member + 1, count - 1))
        out = [list(part) for part in acc]
        for b in range(VARS):
            both = state_ref[member, cell, b].astype(F32)
            real, imag = both[0], both[1]
            total = real + imag
            for part, base in zip(out, bases):
                for a in range(VARS):
                    offset = base + (a * VARS + b)
                    part[3 * a] += row(table, 2 * offset) * real
                    part[3 * a + 1] += row(table, 2 * offset + 1) * imag
                    part[3 * a + 2] += row(sums, offset) * total
        return tuple(tuple(part) for part in out), following

    unroll = 2 if count % 2 == 0 else 1
    return lax.fori_loop(0, count, body, (acc, places(0)), unroll=unroll)[0]


def flux_sum(groups, states, harm_ref, coup_ref, table, sums, start_ref, out_ref):
    harm = lax.axis_index("harm")
    own_count, cells = out_ref.shape[:2]
    width = 2 if own_count % 2 == 0 else 1
    zero = jnp.zeros((8, 128), F32)

    def opening(slot, cell):
        if start_ref is None:
            return (zero,) * (3 * VARS)
        parts = [(start_ref[slot, cell, a, 0], start_ref[slot, cell, a, 1]) for a in range(VARS)]
        return sum(((real, zero, real + imag) for real, imag in parts), ())

    def chunk(step, _):
        cell = step % cells
        first = (step // cells) * width
        acc = tuple(opening(first + place, cell) for place in range(width))
        for shift, state_ref in zip(groups, states):
            acc = flux_block(
                harm * own_count + first, (harm ^ shift) * own_count, harm_ref, coup_ref, state_ref,
                table, sums, range(width), cell, cells, acc,
            )
        for place in range(width):
            for a in range(VARS):
                one, two, three = acc[place][3 * a : 3 * a + 3]
                real = one - two
                imag = three - one - two
                out_ref[first + place, cell, a, 0] = real.astype(out_ref.dtype)
                out_ref[first + place, cell, a, 1] = imag.astype(out_ref.dtype)
        return 0

    lax.fori_loop(0, cells * (own_count // width), chunk, 0)


def first_kernel(
    jac_hbm, state_hbm, harm_hbm, coup_hbm, out_ref, table, sums, harm_ref, coup_ref,
    jac, own, jac_sem, sem,
):
    rows = jac_hbm.size // 128
    flat = jac_hbm.reshape(rows, 128)
    step = -(-rows // (16 * PIECES)) * 16
    spans = [(start, min(step, rows - start)) for start in range(0, rows, step)]
    copies = [
        pltpu.make_async_copy(flat.at[pl.ds(start, size)], jac.at[pl.ds(start, size)], jac_sem.at[i])
        for i, (start, size) in enumerate(spans)
    ]
    others = [
        pltpu.make_async_copy(source, target, sem.at[i])
        for i, (source, target) in enumerate(((harm_hbm, harm_ref), (coup_hbm, coup_ref), (state_hbm, own)))
    ]
    for copy in copies + others:
        copy.start()
    for copy, (start, size) in zip(copies, spans):
        copy.wait()
        for at in range(start, start + size, 16):
            table[pl.ds(at, 16), :] = jac[pl.ds(at, 16), :].astype(F32)
        for at in range(start // 2, (start + size) // 2, 8):
            real = table[pl.ds(2 * at, 8, stride=2), :]
            imag = table[pl.ds(2 * at + 1, 8, stride=2), :]
            sums[pl.ds(at, 8), :] = real + imag
    for copy in others:
        copy.wait()
    flux_sum((0,), (own,), harm_ref, coup_ref, table, sums, None, out_ref)


def next_kernel(groups, harm_ref, coup_ref, *refs):
    states = refs[: len(groups)]
    table, sums, start_ref, out_ref = refs[len(groups) :]
    flux_sum(groups, states, harm_ref, coup_ref, table, sums, start_ref, out_ref)


def local_kernel(harm_total, harm_ref, flux_ref, state_ref, source_ref, out_ref, table):
    own_count, cells = flux_ref.shape[:2]
    first = lax.axis_index("harm") * own_count
    table[: source_ref.shape[0], :] = source_ref[...].astype(F32)

    def body(slot, _):
        spin = harm_ref[first + slot].astype(F32) / harm_total
        for cell in range(cells):
            vec = [state_ref[slot, cell, b].astype(F32) for b in range(VARS)]
            for a in range(VARS):
                real = -spin * vec[a][1]
                imag = spin * vec[a][0]
                for step, weight in ((-2, 1 / 12), (-1, -8 / 12), (1, 8 / 12), (2, -1 / 12)):
                    if 0 <= cell + step < cells:
                        other = flux_ref[slot, cell + step, a].astype(F32)
                        real = real + weight * other[0]
                        imag = imag + weight * other[1]
                for b in range(VARS):
                    weight = row(table, (cell * VARS + a) * VARS + b)
                    real = real + weight * vec[b][0]
                    imag = imag + weight * vec[b][1]
                out_ref[slot, cell, a, 0] = real
                out_ref[slot, cell, a, 1] = imag
        return 0

    lax.fori_loop(0, own_count, body, 0)


def halo_term(ref, on_left, slot, cell, cells, a):
    total = None
    for step, weight in ((-2, 1 / 12), (-1, -8 / 12), (1, 8 / 12), (2, -1 / 12)):
        place = cell + step - (-cells if on_left else cells)
        if 0 <= place < cells and (step < 0) == on_left:
            term = weight * ref[slot, place, a].astype(F32)
            total = term if total is None else total + term
    return 0.0 if total is None else total


def far_first(harm):
    return harm % 4 == 1


def near_kernel(local_ref, near_ref, out_ref):
    own_count, cells = out_ref.shape[:2]
    odd = (lax.axis_index("gx") + far_first(lax.axis_index("harm")).astype(jnp.int32)) % 2
    for side in range(2):

        @pl.when(odd == side)
        def _():
            for slot in range(own_count):
                for cell in range(cells):
                    for a in range(VARS):
                        out_ref[slot, cell, a] = local_ref[slot, cell, a] + halo_term(
                            near_ref, side == 1, slot, cell, cells, a
                        )


def final_kernel(local_ref, far_ref, out_hbm, out_ref, sem):
    own_count, cells = out_ref.shape[:2]

    def put(slot):
        return pltpu.make_async_copy(out_ref.at[slot], out_hbm.at[slot], sem.at[slot])

    odd = (lax.axis_index("gx") + far_first(lax.axis_index("harm")).astype(jnp.int32)) % 2
    for side in range(2):

        @pl.when(odd == side)
        def _():
            for slot in range(own_count):
                for cell in range(cells):
                    for a in range(VARS):
                        total = local_ref[slot, cell, a] + halo_term(
                            far_ref, side == 0, slot, cell, cells, a
                        )
                        out_ref[slot, cell, a] = total.astype(out_ref.dtype)
                put(slot).start()

    for slot in range(own_count):
        put(slot).wait()


def call(kernel, out, spaces, flops, scratch=()):
    return pl.pallas_call(
        kernel,
        out_shape=out,
        in_specs=[pl.BlockSpec(memory_space=space) for space in spaces],
        out_specs=jax.tree.map(lambda x: pl.BlockSpec(memory_space=getattr(x, 'memory_space', VMEM)), out),
        scratch_shapes=scratch,
        compiler_params=pltpu.CompilerParams(vmem_limit_bytes=LIMIT),
        cost_estimate=pl.CostEstimate(flops=flops, bytes_accessed=0, transcendentals=0),
    )


def body(states, jacobian, source, coupling, harmonic_of_slot):
    shape = states.shape
    own_count, cells = shape[:2]
    harms = lax.axis_size("harm")
    planes = lax.axis_size("gx")
    pairs = jacobian.shape[0] * cells * VARS * VARS
    padded = -(-2 * pairs // 16) * 16
    dma = pltpu.SemaphoreType.DMA
    shaped = jax.ShapeDtypeStruct

    def swap(block, shift):
        return lax.ppermute(block, "harm", [(i, i ^ shift) for i in range(harms)])

    work = 2 * VARS * VARS * 6 * own_count * states.size // (2 * VARS)
    even = [shift for shift in range(2, harms, 2)]
    odd = [shift + 1 for shift in even]
    partner = swap(states, 1)
    even_states = [swap(states, shift) for shift in even]
    inputs = (jacobian, states, harmonic_of_slot, coupling)
    part, table, sums, held_harm, held_coup = call(
        first_kernel,
        (
            shaped(shape, F32),
            shaped((padded, 128), F32),
            shaped((padded // 2, 128), F32),
            pltpu.SMEM(harmonic_of_slot.shape, jnp.int32),
            pltpu.SMEM(coupling.shape, jnp.int32),
        ),
        [HBM] * 4,
        work,
        [
            pltpu.VMEM((padded, 128), jacobian.dtype),
            pltpu.VMEM(shape, states.dtype),
            dma((PIECES,)),
            dma((3,)),
        ],
    )(*[pltpu.with_memory_space_constraint(x, HBM) for x in inputs])

    def more(groups, blocks, part, dtype):
        return call(
            functools.partial(next_kernel, groups),
            shaped(shape, dtype),
            [SMEM] * 2 + [VMEM] * (len(groups) + 3),
            work * len(groups),
        )(held_harm, held_coup, *blocks, table, sums, part)

    part = more([1], [partner], part, F32)
    *even_states, part = lax.optimization_barrier((*even_states, part))
    odd_states = [swap(block, 1) for block in even_states]

    part = more(even, even_states, part, F32)
    flux = more(odd, odd_states, part, states.dtype)

    def halo(first):
        pairs = []
        for harm in range(harms):
            for plane in range(planes):
                if far_first(harm) != first:
                    other = plane ^ 1
                else:
                    other = (plane + 1) % planes if plane % 2 else (plane - 1) % planes
                pairs.append((harm * planes + plane, harm * planes + other))
        return lax.ppermute(flux, ("harm", "gx"), pairs)

    near = halo(True)
    far = halo(False)
    sources = cells * VARS * VARS
    local = call(
        functools.partial(local_kernel, coupling.shape[0]),
        shaped(shape, F32),
        [SMEM] + [VMEM] * 3,
        work // 4,
        [pltpu.VMEM((-(-sources // 8) * 8 + 8, 128), F32)],
    )(held_harm, flux, states, source.reshape(sources, 128))
    local = call(near_kernel, shaped(shape, F32), [VMEM] * 2, work // 8)(local, near)
    return call(
        final_kernel,
        HBM(shape, states.dtype),
        [VMEM] * 2,
        work // 8,
        [pltpu.VMEM(shape, states.dtype), dma((own_count,))],
    )(local, far)


def solution(mesh):
    return jax.shard_map(
        body,
        mesh=mesh,
        in_specs=(
            P("harm", "gx", None, None, None, None),
            P(None, "gx", None, None, None, None),
            P("gx", None, None, None),
            P(),
            P(),
        ),
        out_specs=P("harm", "gx", None, None, None, None),
        check_vma=False,
    )
```
